512 devices in a mesh: gz: 128 (over y, z, core), gx: 4 (over x).
Axes of the slice: x: 4, y: 8, z: 8, core: 2. Of those that a mesh axis runs over, the one named last changes fastest.
Arguments:
- velocity: float32 [3, 6, 2048, 4096], P(None, None, 'gz', 'gx'), may hold values from -6 to 6
- colormap: float32 [8, 16, 4], replicated, may hold values from 0 to 1
- map_choice: int32 [4, 4096], P(None, 'gx'), may hold values from 0 to 7
Outputs:
- image: float32 [4, 4, 4096], P(None, None, ('gx', 'gz'))
The draws below stay inside these ranges and needn't reach their ends.
All inputs are finite; a program needn't handle non-finite values.
Results may differ from the reference program's by a relative error of at most 0.0003.
Values sent between devices are 32-bit elements; how exact they have to be, the bound alone decides.
No kernel may reach another device: no remote copies, remote signals or barrier semaphores. Data moves between devices by JAX's collectives and lax.ppermute only.
A program may use at most 64 MiB of HBM per device.

```python
import jax
import jax.numpy as jnp
from jax import lax

BAND = 4
ZD = 16
KNOTS = 16
MAPS = 8
NZ = 2048
NX = 4096
N_GZ = 128


def with_ends(drawn, key, least, largest):
    index_at = [jax.random.randint(jax.random.fold_in(key, axis), (), 0, length) for axis, length in enumerate(drawn.shape)]
    main_axis = drawn.shape.index(max(drawn.shape))
    next_to = index_at[:main_axis] + [(index_at[main_axis] + 1) % drawn.shape[main_axis]] + index_at[main_axis + 1:]
    return drawn.at[tuple(index_at)].set(least).at[tuple(next_to)].set(largest)


def block_scale(rng, shape, pieces, low, top_value):
    def one(axis_at, parts):
        steps = jax.random.uniform(jax.random.fold_in(jax.random.fold_in(rng, 6), axis_at), (parts,), jnp.float32, low / len(pieces), top_value / len(pieces))
        return jnp.repeat(jnp.exp(steps), shape[axis_at] // parts).reshape((-1,) + (1,) * (len(shape) - axis_at - 1))

    factor_of = one(*pieces[0])
    for cut in pieces[1:]:
        factor_of = factor_of * one(*cut)
    return factor_of


def normal_values(rng, shape, width, reach, split=(), held_as=jnp.bfloat16):
    gain = block_scale(rng, shape, split, -0.22, 0.18) if split else 1.0
    drawn = jax.random.normal(rng, shape, jnp.float32) * width * gain
    return jnp.minimum(jnp.maximum(drawn, -reach), reach).astype(held_as)


def setup_inputs(seed: int = 0) -> dict:
    key_of = jax.random.split(jax.random.key(seed), 4)
    return {
        "velocity": normal_values(key_of[0], (3, BAND + 2, NZ, NX), 1.0, 6.0, ((2, 128), (3, 4)), jnp.float32),
        "colormap": jnp.clip(jax.random.uniform(key_of[1], (MAPS, KNOTS, 4), jnp.float32, 0.0, 1.0), 0.0, 1.0),
        "map_choice": with_ends(jax.random.randint(key_of[2], (BAND, NX), 0, MAPS), jax.random.fold_in(key_of[2], 1), 0, MAPS - 1).astype(jnp.int32),
    }


def shade(padded, palette, depth_total):
    along_y = (padded[:, 2:, 1:-1, 1:-1] - padded[:, :-2, 1:-1, 1:-1]) * 0.5
    along_z = (padded[:, 1:-1, 2:, 1:-1] - padded[:, 1:-1, :-2, 1:-1]) * 0.5
    along_x = (padded[:, 1:-1, 1:-1, 2:] - padded[:, 1:-1, 1:-1, :-2]) * 0.5
    derivs = (along_x, along_y, along_z)
    criterion = jnp.zeros_like(along_x[0])
    for component in range(3):
        for direction in range(3):
            criterion = criterion + derivs[direction][component] * derivs[component][direction]
    criterion = -0.5 * criterion
    knot_count = palette.shape[0]
    position = (knot_count - 1) * jax.nn.sigmoid(criterion)
    colours = [jnp.zeros_like(criterion) for channel in range(4)]
    for knot_index in range(knot_count):
        weight = jnp.maximum(0.0, 1.0 - jnp.abs(position - knot_index))
        for channel in range(4):
            colours[channel] = colours[channel] + weight * palette[knot_index, channel][:, None, :]
    kept = jnp.exp(-4.0 * colours[3] / depth_total)
    running = jnp.cumprod(kept, axis=1)
    before = jnp.concatenate([jnp.ones_like(running[:, :1]), running[:, :-1]], axis=1)
    weight_z = before * (1.0 - kept)
    colour = jnp.stack([jnp.sum(weight_z * colours[channel], axis=1) for channel in range(3)])
    return colour, running[:, -1, :]


def reference(velocity, colormap, map_choice):
    palette = jnp.transpose(colormap[map_choice], (2, 3, 0, 1))
    offsets = jnp.arange(ZD + 2, dtype=jnp.int32)

    def one_slab(carry, slab_index):
        accumulated, through = carry
        planes = ((slab_index * ZD - 1 + offsets) % NZ).astype(jnp.int32)
        block = jnp.take(velocity, planes, axis=2)
        block = jnp.concatenate([block[..., -1:], block, block[..., :1]], axis=3)
        colour, slab_kept = shade(block, palette, NZ)
        return (accumulated + through[None] * colour, through * slab_kept), None

    start_state = (jnp.zeros((3, BAND, NX), jnp.float32), jnp.ones((BAND, NX), jnp.float32))
    (accumulated, through), unused = lax.scan(one_slab, start_state, jnp.arange(N_GZ, dtype=jnp.int32))
    return jnp.concatenate([accumulated, (1.0 - through)[None]], axis=0)
```

```python
import jax
import jax.numpy as jnp
from jax import lax
from jax.sharding import PartitionSpec as P


def shift(x, axis, step):
    count = lax.axis_size(axis)
    return lax.ppermute(x, axis, [(i, (i + step) % count) for i in range(count)])


def shade(velocity, z_low, z_high, x_low, x_high, palette, depth_total):
    mid = velocity[:, 1:-1]
    along_y = (velocity[:, 2:] - velocity[:, :-2]) * 0.5
    in_z = jnp.concatenate([z_low, mid, z_high], axis=2)
    along_z = (in_z[:, :, 2:] - in_z[:, :, :-2]) * 0.5
    in_x = jnp.concatenate([x_low, mid, x_high], axis=3)
    along_x = (in_x[..., 2:] - in_x[..., :-2]) * 0.5
    derivs = (along_x, along_y, along_z)
    criterion = jnp.zeros_like(along_x[0])
    for component in range(3):
        for direction in range(3):
            criterion = criterion + derivs[direction][component] * derivs[component][direction]
    criterion = -0.5 * criterion
    knot_count = palette.shape[0]
    position = (knot_count - 1) * jax.nn.sigmoid(criterion)
    colours = [jnp.zeros_like(criterion) for channel in range(4)]
    for knot_index in range(knot_count):
        weight = jnp.maximum(0.0, 1.0 - jnp.abs(position - knot_index))
        for channel in range(4):
            colours[channel] = colours[channel] + weight * palette[knot_index, channel][:, None, :]
    kept = jnp.exp(-4.0 * colours[3] / depth_total)
    before = jnp.ones_like(kept[:, 0])
    colour = [jnp.zeros_like(before) for channel in range(3)]
    for z in range(kept.shape[1]):
        weight_z = before * (1.0 - kept[:, z])
        for channel in range(3):
            colour[channel] = colour[channel] + weight_z * colours[channel][:, z]
        before = before * kept[:, z]
    return jnp.stack(colour + [before])


def on_device(velocity, colormap, map_choice):
    slabs = lax.axis_size("gz")
    depth_total = velocity.shape[2] * slabs
    map_count = colormap.shape[0]
    mid = velocity[:, 1:-1]
    z_low = shift(mid[:, :, -1:], "gz", 1)
    z_high = shift(mid[:, :, :1], "gz", -1)
    x_low = shift(mid[..., -1:], "gx", 1)
    x_high = shift(mid[..., :1], "gx", -1)
    selector = (map_choice[:, :, None] == jnp.arange(map_count, dtype=jnp.int32)).astype(
        jnp.float32
    )
    flat_rows = jnp.dot(
        selector.reshape(-1, map_count),
        colormap.reshape(map_count, -1),
        precision=lax.Precision.HIGHEST,
        preferred_element_type=jnp.float32,
    )
    palette = jnp.transpose(flat_rows.reshape(map_choice.shape + colormap.shape[1:]), (2, 3, 0, 1))
    terms = shade(velocity, z_low, z_high, x_low, x_high, palette, depth_total)
    channels, rows, columns = terms.shape
    share = columns // slabs
    parts = terms.reshape(channels * rows, slabs, share).transpose(1, 0, 2)
    parts = parts.reshape(slabs, channels * rows * share)
    seen = lax.all_to_all(parts, "gz", 0, 0, tiled=True).reshape(slabs, channels, rows * share)
    ahead = jnp.cumprod(seen[:, 3], axis=0)
    before = jnp.concatenate([jnp.ones_like(ahead[:1]), ahead[:-1]], axis=0)
    image = jnp.sum(before[:, None] * seen[:, :3], axis=0)
    image = jnp.concatenate([image, 1.0 - ahead[-1:]], axis=0)
    return image.reshape(channels, rows, share)


def solution(mesh):
    placed = (P(None, None, "gz", "gx"), P(), P(None, "gx"))
    return jax.shard_map(
        on_device,
        mesh=mesh,
        in_specs=placed,
        out_specs=P(None, None, ("gx", "gz")),
        check_vma=False,
    )
```

```python
import functools

import jax
import jax.numpy as jnp
from jax import lax
from jax.experimental import pallas as pl
from jax.experimental.pallas import tpu as pltpu
from jax.sharding import PartitionSpec as P

LANES = 128
TILE = 8
CHUNK = 4


def shift(x, axis, step):
    count = lax.axis_size(axis)
    return lax.ppermute(x, axis, [(i, (i + step) % count) for i in range(count)])


def iota(shape, dim):
    return lax.broadcasted_iota(jnp.int32, shape, dim)


def gather(table, index):
    return jnp.take_along_axis(table, index, axis=1, mode="promise_in_bounds")


def edges_kernel(rate, v_ref, colormap_ref, pad_ref, zhi_ref, zlo_ref, xhi_ref, xlo_ref, table_ref, sem):
    planes, blocks = v_ref.shape[0], v_ref.shape[1]
    tall = planes // 3
    rows = tall // 2 - 2
    inner = pl.ds(1, blocks)
    copy = pltpu.make_async_copy(v_ref, pad_ref.at[:, inner], sem)
    copy.start()
    maps, knots = colormap_ref.shape[0], colormap_ref.shape[2]
    values = jnp.concatenate([colormap_ref[m] for m in range(maps)], axis=1)
    channel, lane = iota(values.shape, 0), iota(values.shape, 1)
    values = jnp.where(channel == 3, values * -rate, values)
    slopes = jnp.where(lane % knots == knots - 1, 0.0, pltpu.roll(values, LANES - 1, 1) - values)
    table_ref[...] = jnp.concatenate([values, slopes], axis=0)
    lane = iota((TILE, LANES), 1)
    flat = pad_ref.reshape(planes * (blocks + 2) * TILE, LANES)
    across = lambda plane, z: flat[pl.ds((plane * (blocks + 2) + 1) * TILE + z, blocks, stride=TILE), :]
    copy.wait()
    xhi = jnp.zeros((TILE, LANES), jnp.float32)
    xlo = jnp.zeros((TILE, LANES), jnp.float32)
    for c in range(3):
        for r in range(rows):
            k = c * rows + r
            first = c * tall + 2 * (r + 1)
            zlo_ref[k] = across(first, 0)
            zhi_ref[k] = across(first + 1, TILE - 1)
            for t in range(2):
                spot = 2 * k + t
                xhi = jnp.where(lane == spot, pltpu.roll(pad_ref[first + t, blocks], spot + 1, 1), xhi)
                xlo = jnp.where(lane == spot, pltpu.roll(pad_ref[first + t, 1], spot, 1), xlo)
    xhi_ref[...] = xhi
    xlo_ref[...] = xlo


def shade_kernel(knots, pad_in, zl_ref, zh_ref, xl_ref, xh_ref, table_ref, map_ref, out_ref, pad_ref, y_ref, t_ref):
    planes, blocks = pad_ref.shape[0], pad_ref.shape[1] - 2
    tall = planes // 3
    rows, depth = tall // 2 - 2, 2 * TILE
    terms = 4 * rows
    lane = iota((TILE, LANES), 1)
    tables = [jnp.broadcast_to(table_ref[k : k + 1, :], (TILE, LANES)) for k in range(8)]
    for k in range(6 * rows):
        plane = (k // (2 * rows)) * tall + 2 * ((k // 2) % rows + 1) + k % 2
        pad_ref[plane, 0] = pltpu.roll(xl_ref[...], LANES - 1 - k, 1)
        pad_ref[plane, blocks + 1] = pltpu.roll(xh_ref[...], (LANES - k) % LANES, 1)

    flat = pad_ref.reshape(planes * (blocks + 2) * TILE, LANES)

    def at(c, y, z, move=0):
        plane = c * tall + 2 * y + z // TILE
        return flat[pl.ds((plane * (blocks + 2) + 1 + move) * TILE + z % TILE, blocks, stride=TILE), :]

    def deep(c, r, z):
        if z < 0:
            return zl_ref[c * rows + r]
        if z == depth:
            return zh_ref[c * rows + r]
        return at(c, r + 1, z)

    last, first = lane == LANES - 1, lane == 0
    half = 0.5 * (knots - 1)
    for r in range(rows):
        offset = map_ref[r] * knots
        sums = [jnp.zeros((TILE, LANES), jnp.float32) for k in range(3)]
        log_light = jnp.zeros((TILE, LANES), jnp.float32)
        light = jnp.ones((TILE, LANES), jnp.float32)
        for start in range(0, depth, CHUNK):
            zs = range(start, start + CHUNK)
            dx, dy, dz = [], [], []
            for c in range(3):
                own = [at(c, r + 1, z) for z in zs]
                left = [jnp.where(last, at(c, r + 1, z, -1), u) for z, u in zip(zs, own)]
                right = [jnp.where(first, at(c, r + 1, z, 1), u) for z, u in zip(zs, own)]
                left = [pltpu.roll(u, 1, 1) for u in left]
                right = [pltpu.roll(u, LANES - 1, 1) for u in right]
                dx.append([b - a for a, b in zip(left, right)])
                dy.append([at(c, r + 2, z) - at(c, r, z) for z in zs])
                dz.append([deep(c, r, z + 1) - deep(c, r, z - 1) for z in zs])
            n = range(CHUNK)
            square = [dx[0][i] * dx[0][i] + dy[1][i] * dy[1][i] + dz[2][i] * dz[2][i] for i in n]
            cross = [dx[1][i] * dy[0][i] + dx[2][i] * dz[0][i] + dy[2][i] * dz[1][i] for i in n]
            total = [a + (b + b) for a, b in zip(square, cross)]
            position = [half + half * jnp.tanh(a * -0.0625) for a in total]
            knot = [a.astype(jnp.int32) for a in position]
            part = [a - k.astype(jnp.float32) for a, k in zip(position, knot)]
            index = [k + offset for k in knot]
            base = [[gather(tables[k], i) for k in range(4)] for i in index]
            slope = [[gather(tables[4 + k], i) for k in range(4)] for i in index]
            shades = [[b + p * s for b, s in zip(bs, ss)] for bs, ss, p in zip(base, slope, part)]
            for i in n:
                log_light = log_light + shades[i][3]
                behind = jnp.exp(log_light)
                weight = light - behind
                light = behind
                sums = [a + weight * s for a, s in zip(sums, shades[i])]
        for k, value in enumerate(sums + [log_light]):
            y_ref[:, k * rows + r, :] = value
    t_ref[...] = y_ref[...].reshape(LANES, LANES).T
    share = LANES // terms
    parts = [t_ref[pl.ds(j, terms, stride=share), :] for j in range(share)]
    group = iota((terms, LANES), 1) // terms
    bit = share // 2
    while bit:
        for j in range(share):
            if j & bit:
                continue
            one, two = parts[j], parts[j + bit]
            clear = (group & bit) == 0
            parts[j] = jnp.where(clear, one, pltpu.roll(two, bit * terms, 1))
            parts[j + bit] = jnp.where(clear, pltpu.roll(one, LANES - bit * terms, 1), two)
        bit //= 2
    for b in range(blocks):
        out_ref[b * terms : (b + 1) * terms, :] = parts[b]


def compose_kernel(seen_ref, out_ref):
    slabs = seen_ref.shape[0]
    rows = out_ref.shape[1]
    terms = 4 * rows
    share = out_ref.shape[2]
    lane, sub = iota((TILE, LANES), 1), iota((TILE, LANES), 0)
    term = lane % terms
    is_light = term >= 3 * rows
    ahead = jnp.zeros((TILE, LANES), jnp.float32)
    image = jnp.zeros((TILE, LANES), jnp.float32)
    for t in range(slabs // TILE):
        seen = seen_ref[t * TILE : (t + 1) * TILE, :]
        own = jnp.where(is_light, seen, 0.0)
        own = own + pltpu.roll(own, LANES - 2 * rows, 1)
        own = own + pltpu.roll(own, LANES - rows, 1)
        reached = own
        for step in (1, 2, 4):
            reached = reached + jnp.where(sub >= step, pltpu.roll(reached, step, 0), 0.0)
        image = image + jnp.exp(ahead + (reached - own)) * seen
        ahead = ahead + jnp.broadcast_to(reached[TILE - 1 :, :], (TILE, LANES))
    image = jnp.sum(image, axis=0, keepdims=True)
    image = jnp.where(is_light[:1], 1.0 - jnp.exp(ahead[:1]), image)
    image = jnp.broadcast_to(image, (terms, LANES))
    index = (iota((terms, LANES), 1) % share) * terms + iota((terms, LANES), 0)
    image = gather(image, index)
    for k in range(4):
        out_ref[k] = image[k * rows : (k + 1) * rows, :share]


def on_device(velocity, colormap, map_choice):
    slabs = lax.axis_size("gz")
    tall, depth, width = velocity.shape[1:]
    rows = tall - 2
    knots = colormap.shape[1]
    blocks = width // LANES
    planes = 3 * tall * depth // TILE
    rate = 4.0 / (depth * slabs)
    tiles = velocity.reshape(3 * tall, depth // TILE, TILE, blocks, LANES).transpose(0, 1, 3, 2, 4)
    tiles = pltpu.with_memory_space_constraint(tiles.reshape(planes, blocks, TILE, LANES), pltpu.HBM)
    whole = pl.BlockSpec(memory_space=pltpu.VMEM)
    params = pltpu.CompilerParams(vmem_limit_bytes=16 * 2**20)
    f32 = lambda *shape: jax.ShapeDtypeStruct(shape, jnp.float32)
    padded, z_last, z_first, x_last, x_first, table = pl.pallas_call(
        functools.partial(edges_kernel, rate),
        out_shape=(
            f32(planes, blocks + 2, TILE, LANES),
            f32(3 * rows, blocks, LANES),
            f32(3 * rows, blocks, LANES),
            f32(TILE, LANES),
            f32(TILE, LANES),
            f32(TILE, LANES),
        ),
        in_specs=[pl.BlockSpec(memory_space=pltpu.HBM), whole],
        out_specs=(whole,) * 6,
        scratch_shapes=[pltpu.SemaphoreType.DMA],
        compiler_params=params,
        name="edges",
    )(tiles, colormap.transpose(0, 2, 1))
    z_low = shift(z_last, "gz", 1)
    z_high = shift(z_first, "gz", -1)
    x_low = shift(x_last, "gx", 1)
    x_high = shift(x_first, "gx", -1)
    parts, _ = pl.pallas_call(
        functools.partial(shade_kernel, knots),
        out_shape=(f32(slabs, LANES), f32(*padded.shape)),
        in_specs=[whole] * 7,
        out_specs=(whole, whole),
        scratch_shapes=[pltpu.VMEM((blocks, 4 * rows, LANES), jnp.float32), pltpu.VMEM((LANES, LANES), jnp.float32)],
        input_output_aliases={0: 1},
        compiler_params=params,
        name="shade",
    )(padded, z_low, z_high, x_low, x_high, table, map_choice.reshape(rows, blocks, LANES))
    seen = lax.all_to_all(parts, "gz", 0, 0, tiled=True)
    return pl.pallas_call(
        compose_kernel,
        out_shape=f32(4, rows, width // slabs),
        in_specs=[whole],
        out_specs=whole,
        compiler_params=params,
        name="compose",
    )(seen)


def solution(mesh):
    placed = (P(None, None, "gz", "gx"), P(), P(None, "gx"))
    return jax.shard_map(
        on_device,
        mesh=mesh,
        in_specs=placed,
        out_specs=P(None, None, ("gx", "gz")),
        check_vma=False,
    )
```

```python
import functools

import jax
import jax.numpy as jnp
from jax import lax
from jax.experimental import pallas as pl
from jax.experimental.pallas import tpu as pltpu
from jax.sharding import PartitionSpec as P


LANES = 128
TILE = 8
CHUNK = 4


def swap(x, axis, first):
    count = lax.axis_size(axis)
    pairs = [(i % count, (i + 1) % count) for i in range(first, count + first, 2)]
    return lax.ppermute(x, axis, pairs + [(b, a) for a, b in pairs])


def iota(shape, dim):
    return lax.broadcasted_iota(jnp.int32, shape, dim)


def gather(table, index):
    return jnp.take_along_axis(table, index, axis=1, mode="promise_in_bounds")


LEAD, PITCH = 8, 24


def edges_kernel(rate, v_ref, colormap_hbm, map_hbm, pad_ref, z0_ref, z1_ref, x0_ref, x1_ref, table_ref, map_ref, colormap_ref, sem, small):
    planes, blocks = v_ref.shape[0], v_ref.shape[1]
    tall = planes // 6
    rows, depth = tall - 2, 2 * TILE
    copies = [pltpu.make_async_copy(v_ref.at[:, b], pad_ref.at[:, :, LEAD + b, :], sem.at[b]) for b in range(blocks)]
    for copy in copies:
        copy.start()
    few = [
        pltpu.make_async_copy(colormap_hbm, colormap_ref, small.at[0]),
        pltpu.make_async_copy(map_hbm, map_ref, small.at[1]),
    ]
    for copy in few:
        copy.start()
    few[0].wait()
    maps, knots = colormap_ref.shape[0], colormap_ref.shape[2]
    values = jnp.concatenate([colormap_ref[m] for m in range(maps)], axis=1)
    channel, lane = iota(values.shape, 0), iota(values.shape, 1)
    values = jnp.where(channel == 3, values * -rate, values)
    slopes = jnp.where(lane % knots == knots - 1, 0.0, pltpu.roll(values, LANES - 1, 1) - values)
    table_ref[...] = jnp.concatenate([values, slopes], axis=0)
    few[1].wait()
    lane = iota((TILE, LANES), 1)
    flat = pad_ref.reshape(planes * TILE * PITCH, LANES)
    z_even, x_even = lax.axis_index("gz") % 2 == 0, lax.axis_index("gx") % 2 == 0
    for copy in copies:
        copy.wait()
    xhi = jnp.zeros((TILE, LANES), jnp.float32)
    xlo = jnp.zeros((TILE, LANES), jnp.float32)
    for c in range(3):
        for r in range(rows):
            k = c * rows + r
            first = (c * tall + r + 1) * depth * PITCH + LEAD
            zlo = flat[pl.ds(first, blocks), :]
            zhi = flat[pl.ds(first + (depth - 1) * PITCH, blocks), :]
            z0_ref[k] = jnp.where(z_even, zhi, zlo)
            z1_ref[k] = jnp.where(z_even, zlo, zhi)
            for t in range(2):
                spot = 2 * k + t
                start = first + t * TILE * PITCH
                ends = flat[pl.ds(start + blocks - 1, TILE, stride=PITCH), :]
                xhi = jnp.where(lane == spot, pltpu.roll(ends, spot + 1, 1), xhi)
                ends = flat[pl.ds(start, TILE, stride=PITCH), :]
                xlo = jnp.where(lane == spot, pltpu.roll(ends, spot, 1), xlo)
    x0_ref[...] = jnp.where(x_even, xhi, xlo)
    x1_ref[...] = jnp.where(x_even, xlo, xhi)


def shade_kernel(knots, pad_in, z0_ref, z1_ref, x0_ref, x1_ref, table_ref, map_ref, out_ref, pad_ref, y_ref, t_ref, index_ref, part_ref):
    blocks = TILE
    tall = pad_ref.shape[0] // 6
    rows, depth = tall - 2, 2 * TILE
    terms = 4 * rows
    lane = iota((TILE, LANES), 1)
    flat = pad_ref.reshape(pad_ref.shape[0] * TILE * PITCH, LANES)
    tables = [jnp.broadcast_to(table_ref[k : k + 1, :], (TILE, LANES)) for k in range(8)]
    z_even, x_even = lax.axis_index("gz") % 2 == 0, lax.axis_index("gx") % 2 == 0
    xl = jnp.where(x_even, x1_ref[...], x0_ref[...])
    xh = jnp.where(x_even, x0_ref[...], x1_ref[...])
    for k in range(6 * rows):
        start = ((k // (2 * rows)) * tall + (k // 2) % rows + 1) * depth * PITCH + (k % 2) * TILE * PITCH + LEAD
        flat[pl.ds(start - 1, TILE, stride=PITCH), :] = pltpu.roll(xl, LANES - 1 - k, 1)
        flat[pl.ds(start + blocks, TILE, stride=PITCH), :] = pltpu.roll(xh, (LANES - k) % LANES, 1)

    def at(c, y, z, move=0):
        return flat[pl.ds(((c * tall + y) * depth + z) * PITCH + LEAD + move, blocks), :]

    def deep(c, r, z):
        if z < 0:
            return jnp.where(z_even, z1_ref[c * rows + r], z0_ref[c * rows + r])
        if z == depth:
            return jnp.where(z_even, z0_ref[c * rows + r], z1_ref[c * rows + r])
        return at(c, r + 1, z)

    last, first = lane == LANES - 1, lane == 0
    half = 0.5 * (knots - 1)

    def locate(r, zs):
        dx, dy, dz = [], [], []
        for c in range(3):
            own = [at(c, r + 1, z) for z in zs]
            left = [jnp.where(last, at(c, r + 1, z, -1), u) for z, u in zip(zs, own)]
            right = [jnp.where(first, at(c, r + 1, z, 1), u) for z, u in zip(zs, own)]
            left = [pltpu.roll(u, 1, 1) for u in left]
            right = [pltpu.roll(u, LANES - 1, 1) for u in right]
            dx.append([b - a for a, b in zip(left, right)])
            dy.append([at(c, r + 2, z) - at(c, r, z) for z in zs])
            dz.append([deep(c, r, z + 1) - deep(c, r, z - 1) for z in zs])
        n = range(len(zs))
        square = [dx[0][i] * dx[0][i] + dy[1][i] * dy[1][i] + dz[2][i] * dz[2][i] for i in n]
        cross = [dx[1][i] * dy[0][i] + dx[2][i] * dz[0][i] + dy[2][i] * dz[1][i] for i in n]
        total = [a + (b + b) for a, b in zip(square, cross)]
        position = [half + half * jnp.tanh(a * -0.0625) for a in total]
        knot = [a.astype(jnp.int32) for a in position]
        offset = map_ref[pl.ds(r, blocks, stride=rows), :] * knots
        for z, p, k in zip(zs, position, knot):
            part_ref[r, z] = p - k.astype(jnp.float32)
            index_ref[r, z] = k + offset

    def paint(r, zs, state):
        sums, log_light, light = state
        index = [index_ref[r, z] for z in zs]
        part = [part_ref[r, z] for z in zs]
        base = [[gather(tables[k], i) for k in range(4)] for i in index]
        slope = [[gather(tables[4 + k], i) for k in range(4)] for i in index]
        shades = [[b + p * s for b, s in zip(bs, ss)] for bs, ss, p in zip(base, slope, part)]
        for here in shades:
            log_light = log_light + here[3]
            behind = jnp.exp(log_light)
            weight = light - behind
            light = behind
            sums = [a + weight * s for a, s in zip(sums, here)]
        return sums, log_light, light

    zero = jnp.zeros((TILE, LANES), jnp.float32)
    chunks = [range(start, start + CHUNK) for start in range(0, depth, CHUNK)]
    for r in range(rows + 1):
        state = [zero, zero, zero], zero, jnp.ones((TILE, LANES), jnp.float32)
        for zs in chunks:
            if r < rows:
                locate(r, zs)
            if r:
                state = paint(r - 1, zs, state)
        if r:
            for k, value in enumerate(state[0] + [state[1]]):
                y_ref[pl.ds(k * rows + r - 1, blocks, stride=terms), :] = value
    t_ref[...] = y_ref[...].T
    share = LANES // terms
    parts = [t_ref[pl.ds(j, terms, stride=share), :] for j in range(share)]
    group = iota((terms, LANES), 1) // terms
    bit = share // 2
    while bit:
        for j in range(share):
            if j & bit:
                continue
            one, two = parts[j], parts[j + bit]
            clear = (group & bit) == 0
            parts[j] = jnp.where(clear, one, pltpu.roll(two, bit * terms, 1))
            parts[j + bit] = jnp.where(clear, pltpu.roll(one, LANES - bit * terms, 1), two)
        bit //= 2
    for b in range(blocks):
        out_ref[b * terms : (b + 1) * terms, :] = parts[b]


def compose_kernel(seen_ref, out_ref):
    slabs = seen_ref.shape[0]
    rows = out_ref.shape[1]
    terms = 4 * rows
    share = out_ref.shape[2]
    lane, sub = iota((TILE, LANES), 1), iota((TILE, LANES), 0)
    term = lane % terms
    is_light = term >= 3 * rows
    ahead = jnp.zeros((TILE, LANES), jnp.float32)
    image = jnp.zeros((TILE, LANES), jnp.float32)
    for t in range(slabs // TILE):
        seen = seen_ref[t * TILE : (t + 1) * TILE, :]
        own = jnp.where(is_light, seen, 0.0)
        own = own + pltpu.roll(own, LANES - 2 * rows, 1)
        own = own + pltpu.roll(own, LANES - rows, 1)
        reached = own
        for step in (1, 2, 4):
            reached = reached + jnp.where(sub >= step, pltpu.roll(reached, step, 0), 0.0)
        image = image + jnp.exp(ahead + (reached - own)) * seen
        ahead = ahead + jnp.broadcast_to(reached[TILE - 1 :, :], (TILE, LANES))
    image = jnp.sum(image, axis=0, keepdims=True)
    image = jnp.where(is_light[:1], 1.0 - jnp.exp(ahead[:1]), image)
    image = jnp.broadcast_to(image, (terms, LANES))
    index = (iota((terms, LANES), 1) % share) * terms + iota((terms, LANES), 0)
    image = gather(image, index)
    for k in range(4):
        out_ref[k] = image[k * rows : (k + 1) * rows, :share]


def on_device(velocity, colormap, map_choice):
    slabs = lax.axis_size("gz")
    tall, depth, width = velocity.shape[1:]
    rows = tall - 2
    knots = colormap.shape[1]
    blocks = width // LANES
    planes = 3 * tall * depth // TILE
    rate = 4.0 / (depth * slabs)
    tiles = velocity.reshape(3 * tall, depth // TILE, TILE, blocks, LANES).transpose(0, 1, 3, 2, 4)
    tiles = tiles.reshape(planes, blocks, TILE, LANES)
    choice = map_choice.reshape(rows, blocks, LANES).transpose(1, 0, 2).reshape(blocks * rows, LANES)
    hbm = lambda x: pltpu.with_memory_space_constraint(x, pltpu.HBM)
    whole = pl.BlockSpec(memory_space=pltpu.VMEM)
    params = pltpu.CompilerParams(vmem_limit_bytes=16 * 2**20)
    f32 = lambda *shape: jax.ShapeDtypeStruct(shape, jnp.float32)
    padded, z0, z1, x0, x1, table, choice = pl.pallas_call(
        functools.partial(edges_kernel, rate),
        out_shape=(
            f32(planes, TILE, PITCH, LANES),
            f32(3 * rows, blocks, LANES),
            f32(3 * rows, blocks, LANES),
            f32(TILE, LANES),
            f32(TILE, LANES),
            f32(TILE, LANES),
            jax.ShapeDtypeStruct(choice.shape, jnp.int32),
        ),
        in_specs=[pl.BlockSpec(memory_space=pltpu.HBM)] * 3,
        out_specs=(whole,) * 7,
        scratch_shapes=[
            pltpu.VMEM((colormap.shape[0], 4, knots), jnp.float32),
            pltpu.SemaphoreType.DMA((blocks,)),
            pltpu.SemaphoreType.DMA((2,)),
        ],
        compiler_params=params,
        name="edges",
    )(hbm(tiles), hbm(colormap.transpose(0, 2, 1)), hbm(choice))
    x0 = swap(x0, "gx", 0)
    x1 = swap(x1, "gx", 1)
    z1 = swap(z1, "gz", 1)
    z0 = swap(z0, "gz", 0)
    parts, _ = pl.pallas_call(
        functools.partial(shade_kernel, knots),
        out_shape=(f32(slabs, LANES), f32(*padded.shape)),
        in_specs=[whole] * 7,
        out_specs=(whole, whole),
        scratch_shapes=[
            pltpu.VMEM((LANES, LANES), jnp.float32),
            pltpu.VMEM((LANES, LANES), jnp.float32),
            pltpu.VMEM((rows, depth, TILE, LANES), jnp.int32),
            pltpu.VMEM((rows, depth, TILE, LANES), jnp.float32),
        ],
        input_output_aliases={0: 1},
        compiler_params=params,
        name="shade",
    )(padded, z0, z1, x0, x1, table, choice)
    seen = lax.all_to_all(parts, "gz", 0, 0, tiled=True)
    return pl.pallas_call(
        compose_kernel,
        out_shape=f32(4, rows, width // slabs),
        in_specs=[whole],
        out_specs=whole,
        compiler_params=params,
        name="compose",
    )(seen)


def solution(mesh):
    placed = (P(None, None, "gz", "gx"), P(), P(None, "gx"))
    return jax.shard_map(
        on_device,
        mesh=mesh,
        in_specs=placed,
        out_specs=P(None, None, ("gx", "gz")),
        check_vma=False,
    )
```

```python
import functools

import jax
import jax.numpy as jnp
from jax import lax
from jax.experimental import pallas as pl
from jax.experimental.pallas import tpu as pltpu
from jax.sharding import PartitionSpec as P


LANES = 128
TILE = 8
CHUNK = 4


def swap(x, axis, first):
    count = lax.axis_size(axis)
    pairs = [(i % count, (i + 1) % count) for i in range(first, count + first, 2)]
    return lax.ppermute(x, axis, pairs + [(b, a) for a, b in pairs])


def iota(shape, dim):
    return lax.broadcasted_iota(jnp.int32, shape, dim)


def gather(table, index):
    return jnp.take_along_axis(table, index, axis=1, mode="promise_in_bounds")


LEAD, PITCH = 8, 24


def edges_kernel(v_ref, z0_ref, z1_ref, x_out_ref, z_ref, x_ref, z_sem, x_sem):
    tall, blocks = v_ref.shape[1], v_ref.shape[3]
    rows = tall - 2
    inner = pl.ds(1, rows)
    copies = []
    for side in range(2):
        for c in range(3):
            plane = v_ref.at[c, inner, side, :, side * (TILE - 1), :]
            copies.append(pltpu.make_async_copy(plane, z_ref.at[side, c], z_sem.at[side, c]))
            tiles = v_ref.at[c, inner, :, side * (blocks - 1)]
            copies.append(pltpu.make_async_copy(tiles, x_ref.at[side, c], x_sem.at[side, c]))
    for copy in copies:
        copy.start()
    z_even = lax.axis_index("gz") % 2 == 0
    mine, count = lax.axis_index("gx"), lax.axis_size("gx")
    lane = iota((TILE, LANES), 1)
    for copy in copies:
        copy.wait()
    for k in range(3 * rows):
        low, high = z_ref[0, k // rows, k % rows], z_ref[1, k // rows, k % rows]
        z0_ref[k] = jnp.where(z_even, high, low)
        z1_ref[k] = jnp.where(z_even, low, high)
    ends = [jnp.zeros((TILE, LANES), jnp.float32)] * 2
    for k in range(6 * rows):
        for side in range(2):
            tile = pltpu.roll(x_ref[side, k // (2 * rows), k // 2 % rows, k % 2], k + side, 1)
            ends[side] = jnp.where(lane == k, tile, ends[side])
    for g in range(count):
        x_out_ref[g] = jnp.where((mine + 1) % count == g, ends[1], ends[0])


def look_up(total, offset, half):
    position = [half + half * jnp.tanh(a * -0.0625) for a in total]
    knot = [a.astype(jnp.int32) for a in position]
    part = [a - k.astype(jnp.float32) for a, k in zip(position, knot)]
    return [k + offset for k in knot], part


def interpolate(tables, index, part):
    found = [[gather(table, i) for table in tables] for i in index]
    return [[f[k] + p * f[4 + k] for k in range(4)] for f, p in zip(found, part)]


def spread(table_ref):
    return [jnp.broadcast_to(table_ref[k : k + 1, :], (TILE, LANES)) for k in range(8)]


def middle_kernel(rate, v_ref, colormap_hbm, map_hbm, x_in_ref, inner_ref, rest_ref, table_ref, map_ref, pad_ref, index_ref, part_ref, colormap_ref, sem, small):
    tall, blocks = v_ref.shape[1], v_ref.shape[3]
    rows, depth = tall - 2, 2 * TILE
    groups = [range(tall - 2), range(tall - 2, tall)]
    loads = []
    for g, ys in enumerate(groups):
        some = pl.ds(ys[0], len(ys))
        loads.append(
            [
                pltpu.make_async_copy(v_ref.at[:, some, :, b], pad_ref.at[:, some, :, :, LEAD + b, :], sem.at[g, b])
                for b in range(blocks)
            ]
        )
    few = [
        pltpu.make_async_copy(colormap_hbm, colormap_ref, small.at[0]),
        pltpu.make_async_copy(map_hbm, map_ref, small.at[1]),
    ]
    for copy in few:
        copy.start()
    for copies in loads:
        for copy in copies:
            copy.start()
    mine, count = lax.axis_index("gx"), lax.axis_size("gx")
    xl, xh = x_in_ref[(mine + count - 1) % count], x_in_ref[(mine + 1) % count]
    flat = pad_ref.reshape(3 * 2 * tall * TILE * PITCH, LANES)
    for k in range(6 * rows):
        start = ((k // (2 * rows)) * tall + (k // 2) % rows + 1) * depth * PITCH + (k % 2) * TILE * PITCH + LEAD
        flat[pl.ds(start - 1, TILE, stride=PITCH), :] = pltpu.roll(xl, LANES - 1 - k, 1)
        flat[pl.ds(start + blocks, TILE, stride=PITCH), :] = pltpu.roll(xh, (LANES - k) % LANES, 1)
    few[0].wait()
    maps, knots = colormap_ref.shape[0], colormap_ref.shape[2]
    values = jnp.concatenate([colormap_ref[m] for m in range(maps)], axis=1)
    channel, lane = iota(values.shape, 0), iota(values.shape, 1)
    values = jnp.where(channel == 3, values * -rate, values)
    slopes = jnp.where(lane % knots == knots - 1, 0.0, pltpu.roll(values, LANES - 1, 1) - values)
    table_ref[...] = jnp.concatenate([values, slopes], axis=0)
    tables = spread(table_ref)
    few[1].wait()
    lane = iota((TILE, LANES), 1)
    last, first = lane == LANES - 1, lane == 0
    half = 0.5 * (knots - 1)

    def at(c, y, z, move=0):
        return flat[pl.ds(((c * tall + y) * depth + z) * PITCH + LEAD + move, blocks), :]

    def locate(r, zs):
        dx, dy, dz = [], [], []
        for c in range(3):
            own = [at(c, r + 1, z) for z in zs]
            left = [jnp.where(last, at(c, r + 1, z, -1), u) for z, u in zip(zs, own)]
            right = [jnp.where(first, at(c, r + 1, z, 1), u) for z, u in zip(zs, own)]
            left = [pltpu.roll(u, 1, 1) for u in left]
            right = [pltpu.roll(u, LANES - 1, 1) for u in right]
            dx.append([b - a for a, b in zip(left, right)])
            dy.append([at(c, r + 2, z) - at(c, r, z) for z in zs])
            dz.append([None if z in (0, depth - 1) else at(c, r + 1, z + 1) - at(c, r + 1, z - 1) for z in zs])
        n = range(len(zs))
        plane = [dx[0][i] * dx[0][i] + dy[1][i] * dy[1][i] for i in n]
        cross = [dx[1][i] * dy[0][i] for i in n]
        if zs[0] == 0:
            for i, z in enumerate(zs):
                rest_ref[r, i, 0] = plane[i] + (cross[i] + cross[i])
                rest_ref[r, i, 1] = dx[2][i]
                rest_ref[r, i, 2] = dy[2][i]
                for c in range(3):
                    rest_ref[r, i, 3 + c] = at(c, r + 1, abs(z - 1))
            return
        plane = [plane[i] + dz[2][i] * dz[2][i] for i in n]
        cross = [cross[i] + dx[2][i] * dz[0][i] + dy[2][i] * dz[1][i] for i in n]
        total = [a + (b + b) for a, b in zip(plane, cross)]
        offset = map_ref[pl.ds(r, blocks, stride=rows), :] * knots
        index, part = look_up(total, offset, half)
        for z, i, p in zip(zs, index, part):
            index_ref[r, z] = i
            part_ref[r, z] = p

    def paint(r, zs, state):
        sums, log_light, light = state
        shades = interpolate(tables, [index_ref[r, z] for z in zs], [part_ref[r, z] for z in zs])
        for here in shades:
            log_light = log_light + here[3]
            behind = jnp.exp(log_light)
            weight = light - behind
            light = behind
            sums = [a + weight * s for a, s in zip(sums, here)]
        return sums, log_light, light

    zero = jnp.zeros((TILE, LANES), jnp.float32)
    chunks = [range(start, min(start + CHUNK, depth - 1)) for start in range(1, depth - 1, CHUNK)]
    for r in range(rows + 1):
        state = [zero, zero, zero], zero, jnp.ones((TILE, LANES), jnp.float32)
        if r < rows:
            if r % 2 == 0:
                for copy in loads[r // 2]:
                    copy.wait()
            locate(r, (0, depth - 1))
        for zs in chunks:
            if r < rows:
                locate(r, zs)
            if r:
                state = paint(r - 1, zs, state)
        if r:
            for k, value in enumerate(state[0] + [state[1]]):
                inner_ref[r - 1, k] = value


def ends_kernel(knots, z0_ref, z1_ref, inner_ref, rest_ref, table_ref, map_ref, out_ref, y_ref, t_ref):
    rows, blocks = inner_ref.shape[0], inner_ref.shape[2]
    terms = 4 * rows
    tables = spread(table_ref)
    half = 0.5 * (knots - 1)
    z_even = lax.axis_index("gz") % 2 == 0
    every = range(rows)
    total, offset = [], []
    for r in every:
        for side in range(2):
            deep = []
            for c in range(3):
                k = c * rows + r
                halo = jnp.where(z_even, z0_ref[k], z1_ref[k]) if side else jnp.where(z_even, z1_ref[k], z0_ref[k])
                near = rest_ref[r, side, 3 + c]
                deep.append(halo - near if side else near - halo)
            cross = rest_ref[r, side, 1] * deep[0] + rest_ref[r, side, 2] * deep[1]
            total.append(rest_ref[r, side, 0] + deep[2] * deep[2] + (cross + cross))
            offset.append(map_ref[pl.ds(r, blocks, stride=rows), :] * knots)
    index, part = look_up(total, 0, half)
    shades = interpolate(tables, [i + o for i, o in zip(index, offset)], part)
    for r in every:
        front, back = shades[2 * r], shades[2 * r + 1]
        log_front = front[3]
        log_inner = log_front + inner_ref[r, 3]
        log_back = log_inner + back[3]
        past_front, past_inner, past_back = jnp.exp(log_front), jnp.exp(log_inner), jnp.exp(log_back)
        for k in range(3):
            value = (1.0 - past_front) * front[k] + past_front * inner_ref[r, k] + (past_inner - past_back) * back[k]
            y_ref[pl.ds(k * rows + r, blocks, stride=terms), :] = value
        y_ref[pl.ds(3 * rows + r, blocks, stride=terms), :] = log_back
    t_ref[...] = y_ref[...].T
    share = LANES // terms
    parts = [t_ref[pl.ds(j, terms, stride=share), :] for j in range(share)]
    group = iota((terms, LANES), 1) // terms
    bit = share // 2
    while bit:
        for j in range(share):
            if j & bit:
                continue
            one, two = parts[j], parts[j + bit]
            clear = (group & bit) == 0
            parts[j] = jnp.where(clear, one, pltpu.roll(two, bit * terms, 1))
            parts[j + bit] = jnp.where(clear, pltpu.roll(one, LANES - bit * terms, 1), two)
        bit //= 2
    for b in range(blocks):
        out_ref[b * terms : (b + 1) * terms, :] = parts[b]


def compose_kernel(seen_ref, out_ref):
    slabs = seen_ref.shape[0]
    rows = out_ref.shape[1]
    terms = 4 * rows
    share = out_ref.shape[2]
    lane, sub = iota((TILE, LANES), 1), iota((TILE, LANES), 0)
    term = lane % terms
    is_light = term >= 3 * rows
    ahead = jnp.zeros((TILE, LANES), jnp.float32)
    image = jnp.zeros((TILE, LANES), jnp.float32)
    for t in range(slabs // TILE):
        seen = seen_ref[t * TILE : (t + 1) * TILE, :]
        own = jnp.where(is_light, seen, 0.0)
        own = own + pltpu.roll(own, LANES - 2 * rows, 1)
        own = own + pltpu.roll(own, LANES - rows, 1)
        reached = own
        for step in (1, 2, 4):
            reached = reached + jnp.where(sub >= step, pltpu.roll(reached, step, 0), 0.0)
        image = image + jnp.exp(ahead + (reached - own)) * seen
        ahead = ahead + jnp.broadcast_to(reached[TILE - 1 :, :], (TILE, LANES))
    image = jnp.sum(image, axis=0, keepdims=True)
    image = jnp.where(is_light[:1], 1.0 - jnp.exp(ahead[:1]), image)
    image = jnp.broadcast_to(image, (terms, LANES))
    index = (iota((terms, LANES), 1) % share) * terms + iota((terms, LANES), 0)
    image = gather(image, index)
    for k in range(4):
        out_ref[k] = image[k * rows : (k + 1) * rows, :share]


def on_device(velocity, colormap, map_choice):
    slabs = lax.axis_size("gz")
    tall, depth, width = velocity.shape[1:]
    rows = tall - 2
    knots = colormap.shape[1]
    blocks = width // LANES
    rate = 4.0 / (depth * slabs)
    tiles = velocity.reshape(3, tall, 2, TILE, blocks, LANES).transpose(0, 1, 2, 4, 3, 5)
    count = lax.axis_size("gx")
    choice = map_choice.reshape(rows, blocks, LANES).transpose(1, 0, 2).reshape(blocks * rows, LANES)
    hbm = lambda x: pltpu.with_memory_space_constraint(x, pltpu.HBM)
    whole, outside = pl.BlockSpec(memory_space=pltpu.VMEM), pl.BlockSpec(memory_space=pltpu.HBM)
    params = pltpu.CompilerParams(vmem_limit_bytes=16 * 2**20)
    f32 = lambda *shape: jax.ShapeDtypeStruct(shape, jnp.float32)
    z0, z1, x = pl.pallas_call(
        edges_kernel,
        out_shape=(f32(3 * rows, blocks, LANES), f32(3 * rows, blocks, LANES), f32(count, TILE, LANES)),
        in_specs=[outside],
        out_specs=(whole,) * 3,
        scratch_shapes=[
            pltpu.VMEM((2, 3, rows, blocks, LANES), jnp.float32),
            pltpu.VMEM((2, 3, rows, 2, TILE, LANES), jnp.float32),
            pltpu.SemaphoreType.DMA((2, 3)),
            pltpu.SemaphoreType.DMA((2, 3)),
        ],
        compiler_params=params,
        name="edges",
    )(hbm(tiles))
    x = lax.all_to_all(x, "gx", 0, 0, tiled=True)
    z1 = swap(z1, "gz", 1)
    z0 = swap(z0, "gz", 0)
    inner, rest, table, choice = pl.pallas_call(
        functools.partial(middle_kernel, rate),
        out_shape=(
            f32(rows, 4, blocks, LANES),
            f32(rows, 2, 6, blocks, LANES),
            f32(TILE, LANES),
            jax.ShapeDtypeStruct(choice.shape, jnp.int32),
        ),
        in_specs=[outside] * 3 + [whole],
        out_specs=(whole,) * 4,
        scratch_shapes=[
            pltpu.VMEM((3, tall, 2, TILE, PITCH, LANES), jnp.float32),
            pltpu.VMEM((rows, depth, TILE, LANES), jnp.int32),
            pltpu.VMEM((rows, depth, TILE, LANES), jnp.float32),
            pltpu.VMEM((colormap.shape[0], 4, knots), jnp.float32),
            pltpu.SemaphoreType.DMA((2, blocks)),
            pltpu.SemaphoreType.DMA((2,)),
        ],
        compiler_params=params,
        name="middle",
    )(hbm(tiles), hbm(colormap.transpose(0, 2, 1)), hbm(choice), x)
    parts = pl.pallas_call(
        functools.partial(ends_kernel, knots),
        out_shape=f32(slabs, LANES),
        in_specs=[whole] * 6,
        out_specs=whole,
        scratch_shapes=[pltpu.VMEM((LANES, LANES), jnp.float32), pltpu.VMEM((LANES, LANES), jnp.float32)],
        compiler_params=params,
        name="ends",
    )(z0, z1, inner, rest, table, choice)
    seen = lax.all_to_all(parts, "gz", 0, 0, tiled=True)
    return pl.pallas_call(
        compose_kernel,
        out_shape=f32(4, rows, width // slabs),
        in_specs=[whole],
        out_specs=whole,
        compiler_params=params,
        name="compose",
    )(seen)


def solution(mesh):
    placed = (P(None, None, "gz", "gx"), P(), P(None, "gx"))
    return jax.shard_map(
        on_device,
        mesh=mesh,
        in_specs=placed,
        out_specs=P(None, None, ("gx", "gz")),
        check_vma=False,
    )
```

```python
import functools

import jax
import jax.numpy as jnp
from jax import lax
from jax.experimental import pallas as pl
from jax.experimental.pallas import tpu as pltpu
from jax.sharding import PartitionSpec as P


LANES = 128
TILE = 8
CHUNK = 2


def swap(x, axis, first):
    count = lax.axis_size(axis)
    pairs = [(i % count, (i + 1) % count) for i in range(first, count + first, 2)]
    return lax.ppermute(x, axis, pairs + [(b, a) for a, b in pairs])


def iota(shape, dim):
    return lax.broadcasted_iota(jnp.int32, shape, dim)


def gather(table, index):
    return jnp.take_along_axis(table, index, axis=1, mode="promise_in_bounds")


LEAD, PITCH = 4, 16


def edges_kernel(rate, v_ref, colormap_hbm, map_hbm, z0_ref, z1_ref, x_out_hbm, pad_ref, table_ref, map_ref, x_ref, x_send, colormap_ref, z_sem, x_sem, out_sem, sem, small):
    tall, blocks = v_ref.shape[1], v_ref.shape[3]
    rows = tall - 2
    inner = pl.ds(1, rows)

    def tiles(side, c):
        source = v_ref.at[c, inner, :, side * (blocks - 1)]
        return pltpu.make_async_copy(source, x_ref.at[side, c], x_sem.at[side, c])

    def plane(side, c, ref, slot):
        source = v_ref.at[c, inner, side, :, side * (TILE - 1), :]
        return pltpu.make_async_copy(source, ref.at[pl.ds(c * rows, rows)], z_sem.at[slot, c])

    for side in range(2):
        for c in range(3):
            tiles(side, c).start()
    z_even = lax.axis_index("gz") % 2 == 0

    @pl.when(z_even)
    def _():
        for c in range(3):
            plane(0, c, z1_ref, 1).start()
            plane(1, c, z0_ref, 0).start()

    @pl.when(jnp.logical_not(z_even))
    def _():
        for c in range(3):
            plane(1, c, z1_ref, 1).start()
            plane(0, c, z0_ref, 0).start()

    few = [
        pltpu.make_async_copy(colormap_hbm, colormap_ref, small.at[0]),
        pltpu.make_async_copy(map_hbm, map_ref, small.at[1]),
    ]
    loads = [pltpu.make_async_copy(v_ref.at[:, :, :, b], pad_ref.at[:, :, :, :, LEAD + b, :], sem.at[b]) for b in range(blocks)]
    for copy in few + loads:
        copy.start()
    mine, count = lax.axis_index("gx"), lax.axis_size("gx")
    lane = iota((TILE, LANES), 1)
    for side in range(2):
        for c in range(3):
            tiles(side, c).wait()
    ends = [jnp.zeros((TILE, LANES), jnp.float32)] * 2
    for k in range(6 * rows):
        for side in range(2):
            tile = pltpu.roll(x_ref[side, k // (2 * rows), k // 2 % rows, k % 2], k + side, 1)
            ends[side] = jnp.where(lane == k, tile, ends[side])
    for g in range(count):
        x_send[g] = jnp.where((mine + 1) % count == g, ends[1], ends[0])
    out = pltpu.make_async_copy(x_send, x_out_hbm, out_sem)
    out.start()
    few[0].wait()
    maps, knots = colormap_ref.shape[0], colormap_ref.shape[2]
    values = jnp.concatenate([colormap_ref[m] for m in range(maps)], axis=1)
    channel, lane = iota(values.shape, 0), iota(values.shape, 1)
    values = jnp.where(channel == 3, values * -rate, values)
    slopes = jnp.where(lane % knots == knots - 1, 0.0, pltpu.roll(values, LANES - 1, 1) - values)
    table_ref[...] = jnp.concatenate([values, slopes], axis=0)
    for c in range(3):
        plane(0, c, z1_ref, 1).wait()
        plane(1, c, z0_ref, 0).wait()
    for copy in few[1:] + loads:
        copy.wait()
    out.wait()


def look_up(total, offset, half):
    position = [half + half * jnp.tanh(a * -0.0625) for a in total]
    knot = [a.astype(jnp.int32) for a in position]
    part = [a - k.astype(jnp.float32) for a, k in zip(position, knot)]
    return [k + offset for k in knot], part


def interpolate(tables, index, part):
    found = [[gather(table, i) for table in tables] for i in index]
    return [[f[k] + p * f[4 + k] for k in range(4)] for f, p in zip(found, part)]


def spread(table_ref):
    return [jnp.broadcast_to(table_ref[k : k + 1, :], (TILE, LANES)) for k in range(8)]


def middle_kernel(knots, pad_in, table_ref, map_ref, x_in_ref, inner_ref, rest_ref, pad_ref, index_ref, part_ref):
    tall, blocks = pad_ref.shape[1], TILE
    rows, depth = tall - 2, 2 * TILE
    mine, count = lax.axis_index("gx"), lax.axis_size("gx")
    xl, xh = x_in_ref[(mine + count - 1) % count], x_in_ref[(mine + 1) % count]
    flat = pad_ref.reshape(3 * 2 * tall * TILE * PITCH, LANES)
    for k in range(6 * rows):
        start = ((k // (2 * rows)) * tall + (k // 2) % rows + 1) * depth * PITCH + (k % 2) * TILE * PITCH + LEAD
        flat[pl.ds(start - 1, TILE, stride=PITCH), :] = pltpu.roll(xl, LANES - 1 - k, 1)
        flat[pl.ds(start + blocks, TILE, stride=PITCH), :] = pltpu.roll(xh, (LANES - k) % LANES, 1)
    tables = spread(table_ref)
    lane = iota((TILE, LANES), 1)
    last, first = lane == LANES - 1, lane == 0
    half = 0.5 * (knots - 1)

    def at(c, y, z, move=0):
        return flat[pl.ds(((c * tall + y) * depth + z) * PITCH + LEAD + move, blocks), :]

    def locate(r, zs):
        dx, dy, dz = [], [], []
        for c in range(3):
            own = [at(c, r + 1, z) for z in zs]
            left = [jnp.where(last, at(c, r + 1, z, -1), u) for z, u in zip(zs, own)]
            right = [jnp.where(first, at(c, r + 1, z, 1), u) for z, u in zip(zs, own)]
            left = [pltpu.roll(u, 1, 1) for u in left]
            right = [pltpu.roll(u, LANES - 1, 1) for u in right]
            dx.append([b - a for a, b in zip(left, right)])
            dy.append([at(c, r + 2, z) - at(c, r, z) for z in zs])
            dz.append([None if z in (0, depth - 1) else at(c, r + 1, z + 1) - at(c, r + 1, z - 1) for z in zs])
        n = range(len(zs))
        plane = [dx[0][i] * dx[0][i] + dy[1][i] * dy[1][i] for i in n]
        cross = [dx[1][i] * dy[0][i] for i in n]
        if zs[0] == 0:
            for i, z in enumerate(zs):
                rest_ref[r, i, 0] = plane[i] + (cross[i] + cross[i])
                rest_ref[r, i, 1] = dx[2][i]
                rest_ref[r, i, 2] = dy[2][i]
                for c in range(3):
                    rest_ref[r, i, 3 + c] = at(c, r + 1, abs(z - 1))
            return
        plane = [plane[i] + dz[2][i] * dz[2][i] for i in n]
        cross = [cross[i] + dx[2][i] * dz[0][i] + dy[2][i] * dz[1][i] for i in n]
        total = [a + (b + b) for a, b in zip(plane, cross)]
        offset = map_ref[pl.ds(r, blocks, stride=rows), :] * knots
        index, part = look_up(total, offset, half)
        for z, i, p in zip(zs, index, part):
            index_ref[r, z] = i
            part_ref[r, z] = p

    def paint(r, zs, state):
        sums, log_light, light = state
        shades = interpolate(tables, [index_ref[r, z] for z in zs], [part_ref[r, z] for z in zs])
        for here in shades:
            log_light = log_light + here[3]
            behind = jnp.exp(log_light)
            weight = light - behind
            light = behind
            sums = [a + weight * s for a, s in zip(sums, here)]
        return sums, log_light, light

    zero = jnp.zeros((TILE, LANES), jnp.float32)
    chunks = [range(start, min(start + CHUNK, depth - 1)) for start in range(1, depth - 1, CHUNK)]
    for r in range(rows + 1):
        state = [zero, zero, zero], zero, jnp.ones((TILE, LANES), jnp.float32)
        if r < rows:
            locate(r, (0, depth - 1))
        for zs in chunks:
            if r < rows:
                locate(r, zs)
            if r:
                state = paint(r - 1, zs, state)
        if r:
            for k, value in enumerate(state[0] + [state[1]]):
                inner_ref[r - 1, k] = value


def ends_kernel(knots, z0_ref, z1_ref, inner_ref, rest_ref, table_ref, map_ref, out_ref, y_ref, t_ref):
    rows, blocks = inner_ref.shape[0], inner_ref.shape[2]
    terms = 4 * rows
    tables = spread(table_ref)
    half = 0.5 * (knots - 1)
    z_even = lax.axis_index("gz") % 2 == 0
    every = range(rows)
    total, offset = [], []
    for r in every:
        for side in range(2):
            deep = []
            for c in range(3):
                k = c * rows + r
                halo = jnp.where(z_even, z0_ref[k], z1_ref[k]) if side else jnp.where(z_even, z1_ref[k], z0_ref[k])
                near = rest_ref[r, side, 3 + c]
                deep.append(halo - near if side else near - halo)
            cross = rest_ref[r, side, 1] * deep[0] + rest_ref[r, side, 2] * deep[1]
            total.append(rest_ref[r, side, 0] + deep[2] * deep[2] + (cross + cross))
            offset.append(map_ref[pl.ds(r, blocks, stride=rows), :] * knots)
    index, part = look_up(total, 0, half)
    shades = interpolate(tables, [i + o for i, o in zip(index, offset)], part)
    for r in every:
        front, back = shades[2 * r], shades[2 * r + 1]
        log_front = front[3]
        log_inner = log_front + inner_ref[r, 3]
        log_back = log_inner + back[3]
        past_front, past_inner, past_back = jnp.exp(log_front), jnp.exp(log_inner), jnp.exp(log_back)
        for k in range(3):
            value = (1.0 - past_front) * front[k] + past_front * inner_ref[r, k] + (past_inner - past_back) * back[k]
            y_ref[pl.ds(k * rows + r, blocks, stride=terms), :] = value
        y_ref[pl.ds(3 * rows + r, blocks, stride=terms), :] = log_back
    t_ref[...] = y_ref[...].T
    share = LANES // terms
    parts = [t_ref[pl.ds(j, terms, stride=share), :] for j in range(share)]
    group = iota((terms, LANES), 1) // terms
    bit = share // 2
    while bit:
        for j in range(share):
            if j & bit:
                continue
            one, two = parts[j], parts[j + bit]
            clear = (group & bit) == 0
            parts[j] = jnp.where(clear, one, pltpu.roll(two, bit * terms, 1))
            parts[j + bit] = jnp.where(clear, pltpu.roll(one, LANES - bit * terms, 1), two)
        bit //= 2
    for b in range(blocks):
        out_ref[b * terms : (b + 1) * terms, :] = parts[b]


def compose_kernel(seen_ref, out_ref):
    slabs = seen_ref.shape[0]
    rows = out_ref.shape[1]
    terms = 4 * rows
    share = out_ref.shape[2]
    lane, sub = iota((TILE, LANES), 1), iota((TILE, LANES), 0)
    term = lane % terms
    is_light = term >= 3 * rows
    ahead = jnp.zeros((TILE, LANES), jnp.float32)
    image = jnp.zeros((TILE, LANES), jnp.float32)
    for t in range(slabs // TILE):
        seen = seen_ref[t * TILE : (t + 1) * TILE, :]
        own = jnp.where(is_light, seen, 0.0)
        own = own + pltpu.roll(own, LANES - 2 * rows, 1)
        own = own + pltpu.roll(own, LANES - rows, 1)
        reached = own
        for step in (1, 2, 4):
            reached = reached + jnp.where(sub >= step, pltpu.roll(reached, step, 0), 0.0)
        image = image + jnp.exp(ahead + (reached - own)) * seen
        ahead = ahead + jnp.broadcast_to(reached[TILE - 1 :, :], (TILE, LANES))
    image = jnp.sum(image, axis=0, keepdims=True)
    image = jnp.where(is_light[:1], 1.0 - jnp.exp(ahead[:1]), image)
    image = jnp.broadcast_to(image, (terms, LANES))
    index = (iota((terms, LANES), 1) % share) * terms + iota((terms, LANES), 0)
    image = gather(image, index)
    for k in range(4):
        out_ref[k] = image[k * rows : (k + 1) * rows, :share]


def on_device(velocity, colormap, map_choice):
    slabs = lax.axis_size("gz")
    tall, depth, width = velocity.shape[1:]
    rows = tall - 2
    knots = colormap.shape[1]
    blocks = width // LANES
    rate = 4.0 / (depth * slabs)
    tiles = velocity.reshape(3, tall, 2, TILE, blocks, LANES).transpose(0, 1, 2, 4, 3, 5)
    count = lax.axis_size("gx")
    choice = map_choice.reshape(rows, blocks, LANES).transpose(1, 0, 2).reshape(blocks * rows, LANES)
    hbm = lambda x: pltpu.with_memory_space_constraint(x, pltpu.HBM)
    whole, outside = pl.BlockSpec(memory_space=pltpu.VMEM), pl.BlockSpec(memory_space=pltpu.HBM)
    params = pltpu.CompilerParams(vmem_limit_bytes=16 * 2**20)
    f32 = lambda *shape: jax.ShapeDtypeStruct(shape, jnp.float32)
    z0, z1, x, padded, table, choice = pl.pallas_call(
        functools.partial(edges_kernel, rate),
        out_shape=(
            f32(3 * rows, blocks, LANES),
            f32(3 * rows, blocks, LANES),
            f32(count, TILE, LANES),
            f32(3, tall, 2, TILE, PITCH, LANES),
            f32(TILE, LANES),
            jax.ShapeDtypeStruct(choice.shape, jnp.int32),
        ),
        in_specs=[outside] * 3,
        out_specs=(whole, whole, outside, whole, whole, whole),
        scratch_shapes=[
            pltpu.VMEM((2, 3, rows, 2, TILE, LANES), jnp.float32),
            pltpu.VMEM((count, TILE, LANES), jnp.float32),
            pltpu.VMEM((colormap.shape[0], 4, knots), jnp.float32),
            pltpu.SemaphoreType.DMA((2, 3)),
            pltpu.SemaphoreType.DMA((2, 3)),
            pltpu.SemaphoreType.DMA,
            pltpu.SemaphoreType.DMA((blocks,)),
            pltpu.SemaphoreType.DMA((2,)),
        ],
        compiler_params=params,
        name="edges",
    )(hbm(tiles), hbm(colormap.transpose(0, 2, 1)), hbm(choice))
    x = lax.all_to_all(x, "gx", 0, 0, tiled=True)
    z1 = swap(z1, "gz", 1)
    z0 = swap(z0, "gz", 0)
    inner, rest, _ = pl.pallas_call(
        functools.partial(middle_kernel, knots),
        out_shape=(f32(rows, 4, blocks, LANES), f32(rows, 2, 6, blocks, LANES), f32(*padded.shape)),
        in_specs=[whole] * 4,
        out_specs=(whole,) * 3,
        scratch_shapes=[
            pltpu.VMEM((rows, depth, TILE, LANES), jnp.int32),
            pltpu.VMEM((rows, depth, TILE, LANES), jnp.float32),
        ],
        input_output_aliases={0: 2},
        compiler_params=params,
        name="middle",
    )(padded, table, choice, x)
    parts = pl.pallas_call(
        functools.partial(ends_kernel, knots),
        out_shape=f32(slabs, LANES),
        in_specs=[whole] * 6,
        out_specs=whole,
        scratch_shapes=[pltpu.VMEM((LANES, LANES), jnp.float32), pltpu.VMEM((LANES, LANES), jnp.float32)],
        compiler_params=params,
        name="ends",
    )(z0, z1, inner, rest, table, choice)
    seen = lax.all_to_all(parts, "gz", 0, 0, tiled=True)
    return pl.pallas_call(
        compose_kernel,
        out_shape=f32(4, rows, width // slabs),
        in_specs=[whole],
        out_specs=whole,
        compiler_params=params,
        name="compose",
    )(seen)


def solution(mesh):
    placed = (P(None, None, "gz", "gx"), P(), P(None, "gx"))
    return jax.shard_map(
        on_device,
        mesh=mesh,
        in_specs=placed,
        out_specs=P(None, None, ("gx", "gz")),
        check_vma=False,
    )
```
